32 devices in a mesh: shot: 4 (over x, core), slab: 8 (over z, y).
Axes of the slice: x: 2, y: 2, z: 4, core: 2. Of those that a mesh axis runs over, the one named last changes fastest.
Arguments:
- fwd_prev: float32 [4, 256, 128, 128], P('shot', None, 'slab'), may hold values from -6 to 6
- fwd_now: float32 [4, 256, 128, 128], P('shot', None, 'slab'), may hold values from -6 to 6
- adj_late: float32 [4, 256, 128, 128], P('shot', None, 'slab'), may hold values from -6 to 6
- adj_last: float32 [4, 256, 128, 128], P('shot', None, 'slab'), may hold values from -6 to 6
- speed_model: float32 [512, 128, 128], P('shot', 'slab'), may hold values from 0.04 to 0.24
- anchors: int32 [4], replicated, may hold values from 0 to 256
- traces: float32 [8, 1024], P(None, ('shot', 'slab')), may hold values from -6 to 6
- dest: int32 [1024, 1], P(('shot', 'slab')), may hold values from 0 to 31; in each aligned block of 32 rows (0 to 31, 32 to 63, ...) at most 2 rows name the same one
- rec_pos: int32 [1024], P(('shot', 'slab')), may hold values from 0 to 4095
Outputs:
- image: float32 [512, 128, 128], P('shot', 'slab')
The draws below stay inside these ranges and needn't reach their ends.
Inputs may be any that keep to these rules, and one draw needn't show every extreme that they name: `dest`: within the rows of one device (aligned blocks of 32 receivers) no value occurs more than 2 times, and some value occurs exactly 2 times.
All inputs are finite; a program needn't handle non-finite values.
Results may differ from the reference program's by a relative error of at most 0.00002.
Values sent between devices are 32-bit elements; how exact they have to be, the bound alone decides.
A program may use at most 192 MiB of HBM per device.

```python
import math
import jax
import jax.numpy as jnp
import numpy as np
from jax import lax

CX = 16
AY = 256
NZ = 128
NSTEP = 8
CAP = 2
RDEPTH = 3
MX = 128
MY = 512
REC_DEV = 32
NREC = 1024
N_SHOT = 4
N_SLAB = 8
DEVICES = 32


def with_ends(drawn, stream_key, least, top_value):
    place = [jax.random.randint(jax.random.fold_in(stream_key, axis), (), 0, length) for axis, length in enumerate(drawn.shape)]
    widest = drawn.shape.index(max(drawn.shape))
    next_to = place[:widest] + [(place[widest] + 1) % drawn.shape[widest]] + place[widest + 1:]
    return drawn.at[tuple(place)].set(least).at[tuple(next_to)].set(top_value)


def block_scale(own_key, extent, shards, low, high):
    factor_of, own = 1.0, jax.random.fold_in(own_key, 6)
    for position, blocks in shards:
        steps = jnp.exp(jax.random.uniform(jax.random.fold_in(own, position), (blocks,), jnp.float32, low / len(shards), high / len(shards)))
        factor_of = factor_of * jnp.repeat(steps, extent[position] // blocks).reshape([-1 if axis == position else 1 for axis in range(len(extent))])
    return factor_of


def shared_out(stream_key, own, number, rows, number_of, top, reach, slope):
    sequence = jax.random.permutation(stream_key, number_of)
    heavy_load, usual = shares(number_of, rows * top, reach, slope, True), shares(number_of, rows * top, reach, slope, False)
    places = jnp.arange(number_of)

    def named(tallies, offset_by):
        used = int((tallies > 0).sum())
        fixed = max(1, used // 4)
        shifted = fixed + (places - fixed + offset_by * (used - fixed)) % max(1, number_of - fixed)
        return jnp.zeros((number_of,), jnp.int32).at[sequence[jnp.where(places < fixed, places, shifted)]].set(jnp.asarray(tallies, jnp.int32))

    tallies = jnp.where(number % 4 == 0, named(heavy_load, number // 4), named(usual, number - number // 4 - 1))
    mixed = jax.random.permutation(jax.random.fold_in(own, 3), number_of)
    source_of, receiver = mixed[0:number_of // 2 * 2:2], mixed[1:number_of // 2 * 2:2]
    slack = jnp.minimum(tallies[source_of] - 1, reach - tallies[receiver]) // 2
    slack = jnp.where((source_of == sequence[0]) | (receiver == sequence[0]) | (tallies[receiver] == 0), 0, jnp.maximum(slack, 0))
    shifted = jax.random.randint(jax.random.fold_in(own, 4), (number_of // 2,), 0, 1 << 20) % (slack + 1)
    tallies = tallies.at[source_of].add(-shifted).at[receiver].add(shifted)
    members = jnp.searchsorted(jnp.cumsum(tallies), jnp.arange(rows * top), side="right").astype(jnp.int32)
    table = members.reshape(top, rows).T
    table = table[jax.random.permutation(jax.random.fold_in(own, 1), rows)]
    offset_by = jax.random.randint(jax.random.fold_in(own, 2), (rows, 1), 0, top)
    return jnp.take_along_axis(table, (jnp.arange(top)[None, :] + offset_by) % top, axis=1)


def shares(count, total, limit, slope, full):
    portions = [(1 << 20) // math.isqrt(rank ** slope) + 1 for rank in range(1, count + 1)]
    largest = limit if full else min(limit, max(-(-total // count), total * portions[0] // sum(portions)))
    least = 1 if total - largest >= count - 1 else 0
    given, surplus = [largest] + [least] * (count - 1), total - largest - least * (count - 1)
    while surplus > 0:
        candidates = [i for i in range(1, count) if given[i] < largest] or [i for i in range(1, count) if given[i] < limit]
        mass, remaining = sum([portions[i] for i in candidates]), surplus
        for i in candidates:
            addition = min(limit - given[i], max(1, remaining * portions[i] // mass), surplus)
            given[i] = given[i] + addition
            surplus = surplus - addition
    return np.array(given)


def centred(rng, dims, spread, limit, pieces=(), dtype=jnp.bfloat16):
    loudness = block_scale(rng, dims, pieces, -0.22, 0.18) if pieces else 1.0
    array = jax.random.normal(rng, dims, jnp.float32) * spread * loudness
    return jnp.minimum(jnp.maximum(array, -limit), limit).astype(dtype)


def setup_inputs(seed: int = 0) -> dict:
    key_list = jax.random.split(jax.random.key(seed), 10)
    fwd_prev = centred(key_list[0], (N_SHOT, AY, MX, NZ), 1.0, 6.0, ((0, 4), (2, 8)), jnp.float32)
    fwd_now = centred(key_list[1], (N_SHOT, AY, MX, NZ), 1.0, 6.0, ((0, 4), (2, 8)), jnp.float32)
    adj_late = centred(key_list[2], (N_SHOT, AY, MX, NZ), 1.0, 6.0, ((0, 4), (2, 8)), jnp.float32)
    adj_last = centred(key_list[3], (N_SHOT, AY, MX, NZ), 1.0, 6.0, ((0, 4), (2, 8)), jnp.float32)
    speed_model = jnp.clip(jnp.exp(math.log(0.24) - 1.7917595 * jax.random.uniform(key_list[4], (MY, MX, NZ), jnp.float32) ** block_scale(key_list[4], (MY, MX, NZ), ((0, 4), (1, 8)), -0.2, 0.2)), 0.04, 0.24)
    anchors = with_ends(jax.random.randint(key_list[5], (N_SHOT,), 0, MY - AY + 1), jax.random.fold_in(key_list[5], 1), 0, MY - AY).astype(jnp.int32)
    traces = centred(key_list[6], (NSTEP, NREC), 1.0, 6.0, ((1, 32),), jnp.float32)
    dest_keys = jax.random.split(jax.random.fold_in(key_list[7], 1), NREC // REC_DEV)
    dest_turns = jax.random.permutation(jax.random.fold_in(key_list[7], 3), NREC // REC_DEV)
    dest = jax.vmap(lambda own, number: shared_out(jax.random.fold_in(key_list[7], 2), own, number, REC_DEV, DEVICES, 1, CAP, 2))(dest_keys, dest_turns).reshape((NREC, 1))
    rec_pos = with_ends(jax.random.randint(key_list[8], (NREC,), 0, AY * CX), jax.random.fold_in(key_list[8], 1), 0, (AY * CX) - 1).astype(jnp.int32)
    return {"fwd_prev": fwd_prev, "fwd_now": fwd_now, "adj_late": adj_late, "adj_last": adj_last, "speed_model": speed_model, "anchors": anchors, "traces": traces, "dest": dest, "rec_pos": rec_pos}


centre_coef = -2.5
near_coef = 4.0 / 3.0
far_coef = -1.0 / 12.0


def laplace(field):
    padded = jnp.pad(field, ((2, 2), (0, 0), (2, 2)))
    core = padded[2:-2, 2:-2, 2:-2]
    near = padded[1:-3, 2:-2, 2:-2] + padded[3:-1, 2:-2, 2:-2]
    near = near + padded[2:-2, 1:-3, 2:-2] + padded[2:-2, 3:-1, 2:-2]
    near = near + padded[2:-2, 2:-2, 1:-3] + padded[2:-2, 2:-2, 3:-1]
    far = padded[:-4, 2:-2, 2:-2] + padded[4:, 2:-2, 2:-2]
    far = far + padded[2:-2, :-4, 2:-2] + padded[2:-2, 4:, 2:-2]
    far = far + padded[2:-2, 2:-2, :-4] + padded[2:-2, 2:-2, 4:]
    return 3.0 * centre_coef * core + near_coef * near + far_coef * far


def full_laplace(field):
    return laplace(jnp.pad(field, ((0, 0), (2, 2), (0, 0))))


def reference(fwd_prev, fwd_now, adj_late, adj_last, speed_model, anchors, traces, dest, rec_pos):
    image = jnp.zeros((MY, MX, NZ), jnp.float32)
    target = dest[:, 0]
    for shot_index in range(N_SHOT):
        anchor = anchors[shot_index].astype(jnp.int32)
        speed = lax.dynamic_slice_in_dim(speed_model, anchor, AY, 0)
        prev, now = fwd_prev[shot_index], fwd_now[shot_index]
        snaps = []
        for step in range(NSTEP):
            nxt = 2.0 * now - prev + speed * full_laplace(now)
            prev, now = now, nxt
            snaps.append(now)
        chosen = (target // N_SLAB) == shot_index
        column = (target % N_SLAB) * CX + rec_pos % CX
        row = rec_pos // CX
        amounts = jnp.where(chosen[None, :], traces, jnp.float32(0.0))
        planes = jnp.zeros((NSTEP, AY, MX), jnp.float32).at[:, row, column].add(amounts)
        late, last = adj_late[shot_index], adj_last[shot_index]
        partial_value = jnp.zeros((AY, MX, NZ), jnp.float32)
        for level in range(NSTEP, 0, -1):
            drive = full_laplace(last).at[:, :, RDEPTH].add(planes[level - 1])
            current = 2.0 * last - late + speed * drive
            partial_value = partial_value + snaps[level - 1] * current
            late, last = last, current
        window = lax.dynamic_slice_in_dim(image, anchor, AY, 0)
        image = lax.dynamic_update_slice_in_dim(image, window + partial_value, anchor, 0)
    return image
```

```python
import jax
import jax.numpy as jnp
from jax import lax
from jax.experimental import pallas as pl
from jax.experimental.pallas import tpu as pltpu
from jax.sharding import PartitionSpec as P

NSTEP = 8
CAP = 2
RDEPTH = 3
B = 32
SKEW = B // NSTEP
TOP = B + SKEW
DELAY = 8
PIECES = 4
GROUP = 8
LAG_A = 1
LAG_B = 2
SCALE = 12.0

MESH = pl.DeviceIdType.MESH


def snap(n):
    late = (n + NSTEP - 1) // NSTEP
    return (n + 1) * (1 - late) + (n - 1) * late


def place_of(field, k):
    if field == 0:
        return snap(k)
    return NSTEP + (k + 1) % 2


def halo_slot(field, k):
    if field == 0:
        return k
    first = 1 - (k + NSTEP - 1) // NSTEP
    final = (k + 1) // NSTEP
    return k + NSTEP * first + 2 * final


def wave_kernel(
    anchors, now, prev, last, late, speed_in, packet,
    out_ref,
    F, H, E, C, T, M, G, band, gathered,
    load_sem, field_send, field_recv, speed_send, speed_recv,
    halo_send, halo_recv, move_send, move_recv,
    slab_send, slab_recv, shot_send, shot_recv, image_send, image_recv,
):
    count = lax.axis_size("slab")
    shots = lax.axis_size("shot")
    shot = lax.axis_index("shot")
    me = lax.axis_index("slab")
    block = out_ref.shape[0]
    rows = now.shape[0]
    depth = now.shape[3]
    chunks = rows // B
    piece = block // PIECES
    edge_rows = 2 * B
    core = shot % 2
    side_of = me % 2
    home = core == side_of
    role_shot = shot - core + side_of
    role_slab = me - side_of + core
    twin = (role_shot, role_slab)
    partner = shot + 1 - 2 * core
    across = (shot + 2) % 4
    beyond = (partner + 2) % 4
    anchor = anchors[shot]
    left_device = (partner, me - 2 * (1 - core))
    right_device = (partner, me + 2 * core)
    has_left = role_slab > 0
    has_right = role_slab < count - 1
    sources = [now, prev, last, late]
    first_place = [place_of(0, 0), place_of(0, -1), place_of(1, 0), place_of(1, -1)]
    zero_row = jnp.zeros((2, 8, depth), jnp.float32)
    zero_edge = jnp.zeros((8, depth), jnp.float32)

    def field_target(i, c):
        return F.at[first_place[i], pl.ds(TOP + c * B, B)]

    def field_local(i, c):
        return pltpu.make_async_copy(
            sources[i].at[pl.ds(c * B, B)], field_target(i, c), field_recv.at[i, c]
        )

    def field_swap(i, c):
        return pltpu.make_async_remote_copy(
            src_ref=sources[i].at[pl.ds(c * B, B)],
            dst_ref=field_target(i, c),
            send_sem=field_send.at[i, c],
            recv_sem=field_recv.at[i, c],
            device_id=twin,
            device_id_type=MESH,
        )

    def field_arrived(i, c):
        @pl.when(home)
        def _():
            field_local(i, c).wait()

        @pl.when(jnp.logical_not(home))
        def _():
            field_swap(i, c).wait_recv()

    def over(n, act):
        def run(i, carry):
            act(i)
            return carry

        lax.fori_loop(0, n, run, 0)

    own_speed = pltpu.make_async_copy(speed_in, M.at[pl.ds(shot * block, block)], load_sem.at[0])
    own_packet = pltpu.make_async_copy(packet.at[me], gathered.at[shot, me], load_sem.at[1])
    own_packet.start()
    own_speed.start()

    @pl.when(home)
    def _():
        for i in range(4):
            over(chunks, lambda c: field_local(i, c).start())

    barrier = pltpu.get_barrier_semaphore()

    def greet(device):
        pl.semaphore_signal(barrier, inc=1, device_id=device, device_id_type=MESH)

    def greet_slab(offset):
        greet((shot, (me + 1 + offset) % count))

    def greet_shot(offset):
        greet(((shot + 1 + offset) % shots, me))

    over(count - 1, greet_slab)
    over(shots - 1, greet_shot)

    pair = me // 2
    far_pair = pair + 2 * core - 1

    @pl.when(jnp.logical_not(home))
    def _():
        greet(twin)

    @pl.when((far_pair >= 0) & (far_pair < count // 2))
    def _():
        greet((partner, me + 2 * (2 * core - 1)))

    def clear_pads(i):
        for s in range(NSTEP + 2):
            F[s, i] = zero_row

    def clear_below(i):
        for s in range(NSTEP + 2):
            F[s, TOP + rows + i] = zero_row

    over(TOP, clear_pads)
    over(B, clear_below)

    def clear_speed(i):
        C[i] = zero_row

    over(TOP, clear_speed)

    def clear_speed_below(i):
        C[TOP + rows + i] = zero_row

    over(B, clear_speed_below)
    for s in range(4):
        G[s, 0:GROUP] = jnp.zeros((GROUP, 2, 8, depth), jnp.float32)
        G[s, GROUP + rows : 2 * GROUP + rows] = jnp.zeros((GROUP, 2, 8, depth), jnp.float32)
    for s in range(NSTEP + 2):
        k = s if s < NSTEP else (0 if s == NSTEP else NSTEP - 1)
        for side in range(2):
            start = (B - SKEW * (k + 1)) * 2
            H[s, side, start : start + 2 * SKEW] = zero_edge
            if k == 0:
                for g in range(edge_rows // 8):
                    H[s, side, 2 * (B + rows) + 8 * g : 2 * (B + rows) + 8 * g + 8] = zero_edge

    def clear_halo(side):
        def run(i):
            for s in range(NSTEP + 2):
                H[s, side, pl.ds(i * 8, 8)] = zero_edge

        over(H.shape[2] // 8, run)

    @pl.when(jnp.logical_not(has_left))
    def _():
        clear_halo(0)

    @pl.when(jnp.logical_not(has_right))
    def _():
        clear_halo(1)

    line = lax.broadcasted_iota(jnp.int32, (2 * depth, depth), 0)
    column = lax.broadcasted_iota(jnp.int32, (2 * depth, depth), 1)
    apart = (line % depth) - column
    apart = apart * apart
    weight = jnp.where(apart == 1, 16.0, jnp.where(apart == 4, -1.0, 0.0))
    band[...] = weight.astype(jnp.bfloat16)

    pl.semaphore_wait(
        barrier,
        count - 1 + shots - 1
        + jnp.where(home, 0, 1)
        + jnp.where((far_pair >= 0) & (far_pair < count // 2), 1, 0),
    )

    def slab_copy(source, target):
        return pltpu.make_async_remote_copy(
            src_ref=packet.at[target],
            dst_ref=gathered.at[shot, source],
            send_sem=slab_send.at[target],
            recv_sem=slab_recv.at[source],
            device_id=(shot, target),
            device_id_type=MESH,
        )

    def shot_copy(source, target):
        return pltpu.make_async_remote_copy(
            src_ref=gathered.at[source],
            dst_ref=gathered.at[source],
            send_sem=shot_send.at[target],
            recv_sem=shot_recv.at[source],
            device_id=(target, me),
            device_id_type=MESH,
        )

    def over_slabs(act):
        over(count - 1, lambda i: act((me + 1 + i) % count))

    def over_shots(act):
        over(shots - 1, lambda i: act((shot + 1 + i) % shots))

    def move(kind, p, source, target, device):
        return pltpu.make_async_remote_copy(
            src_ref=source,
            dst_ref=target,
            send_sem=move_send.at[kind, p],
            recv_sem=move_recv.at[kind, p],
            device_id=(device, me),
            device_id_type=MESH,
        )

    def model_across(p):
        span = M.at[pl.ds(shot * block + p * piece, piece)]
        return move(0, p, speed_in.at[pl.ds(p * piece, piece)], span, across)

    def model_partner(p):
        span = M.at[pl.ds(shot * block + p * piece, piece)]
        return move(1, p, speed_in.at[pl.ds(p * piece, piece)], span, partner)

    def model_onward(p):
        span = M.at[pl.ds(across * block + p * piece, piece)]
        return move(2, p, span, span, partner)

    def speed_swap(c):
        span = pl.ds(TOP + c * B, B)
        return pltpu.make_async_remote_copy(
            src_ref=T.at[span],
            dst_ref=C.at[span],
            send_sem=speed_send.at[c],
            recv_sem=speed_recv.at[c],
            device_id=twin,
            device_id_type=MESH,
        )

    def transfer(field, k, side, c):
        span = pl.ds(pl.multiple_of((c * B - SKEW * k + B) * 2, 8), edge_rows)
        device = left_device if side == 0 else right_device
        return pltpu.make_async_remote_copy(
            src_ref=E.at[k, side, span],
            dst_ref=H.at[halo_slot(field, k), 1 - side, span],
            send_sem=halo_send.at[field, k, side, c],
            recv_sem=halo_recv.at[field, k, 1 - side, c],
            device_id=device,
            device_id_type=MESH,
        )

    def both_sides(act_left, act_right):
        @pl.when(has_left)
        def _():
            act_left()

        @pl.when(has_right)
        def _():
            act_right()

    def send(field, k, c):
        both_sides(
            lambda: transfer(field, k, 0, c).start(), lambda: transfer(field, k, 1, c).start()
        )

    def sent(field, k, c):
        both_sides(
            lambda: transfer(field, k, 0, c).wait_send(),
            lambda: transfer(field, k, 1, c).wait_send(),
        )

    def receive(field, k, c):
        both_sides(
            lambda: transfer(field, k, 1, c).wait_recv(),
            lambda: transfer(field, k, 0, c).wait_recv(),
        )

    quad = lax.broadcasted_iota(jnp.int32, (B // 4, 8, depth), 1)

    def store_edges(k, c, v0, v1):
        a = v0.reshape(B // 4, 4, 8, depth)
        b = v1.reshape(B // 4, 4, 8, depth)
        low, high = a[:, 0], pltpu.roll(b[:, 0], 2, 1)
        for i in range(1, 4):
            low = jnp.where(quad >= 2 * i, pltpu.roll(a[:, i], 2 * i, 1), low)
            turned = b[:, i] if i == 3 else pltpu.roll(b[:, i], 2 * i + 2, 1)
            high = jnp.where(quad >= 2 * i, turned, high)
        span = pl.ds(pl.multiple_of((c * B - SKEW * k + B) * 2, 8), edge_rows)
        E[k, 0, span] = low.reshape(edge_rows, depth)
        E[k, 1, span] = high.reshape(edge_rows, depth)

    def pack(field, c):
        field_arrived(2 * field, c)
        if field == 1:
            sent(0, 0, c)
        cells = F[first_place[2 * field], pl.ds(TOP + c * B, B)]
        store_edges(0, c, cells[:, 0], cells[:, 1])
        send(field, 0, c)

    sub = lax.broadcasted_iota(jnp.int32, (B, 8, depth), 1)
    lane = lax.broadcasted_iota(jnp.int32, (B, 2, 8, depth), 3)

    def turned(ghost, shift):
        if shift % 8 == 0:
            return ghost
        return pltpu.roll(ghost, shift % 8, 1)

    def spread(ghost, shift):
        parts = [turned(ghost, shift - 2 * i) for i in range(4)]
        return jnp.stack(parts, axis=1).reshape(B, 8, depth)

    def advance(field, k, c):
        base = c * B - SKEW * k
        newer, older, target = place_of(field, k - 1), place_of(field, k - 2), place_of(field, k)

        @pl.when((k > 1) | (c < chunks))
        def _():
            receive(field, k - 1, c)

        if field == 1:
            @pl.when(k < NSTEP)
            def _():
                sent(0, k, c)

        window = F[newer, pl.ds(TOP + base - 2, B + 4)]
        cells = window[2 : B + 2]
        near = window[1 : B + 1] + window[3 : B + 3]
        far = window[0:B] + window[4 : B + 4]
        v0, v1 = cells[:, 0], cells[:, 1]
        span = pl.ds(pl.multiple_of((base + B) * 2, 8), edge_rows)
        slot = halo_slot(field, k - 1)
        left = H[slot, 0, span].reshape(B // 4, 8, depth)
        right = H[slot, 1, span].reshape(B // 4, 8, depth)
        a1, b1 = pltpu.roll(v0, 1, 1), pltpu.roll(v1, 1, 1)
        a2, b2 = pltpu.roll(v0, 2, 1), pltpu.roll(v1, 2, 1)
        a7, b7 = pltpu.roll(v0, 7, 1), pltpu.roll(v1, 7, 1)
        a6, b6 = pltpu.roll(v0, 6, 1), pltpu.roll(v1, 6, 1)
        near0 = near[:, 0] + jnp.where(sub < 1, spread(left, 7), a1) + jnp.where(sub >= 7, b7, a7)
        near1 = near[:, 1] + jnp.where(sub < 1, a1, b1) + jnp.where(sub >= 7, spread(right, 7), b7)
        far0 = far[:, 0] + jnp.where(sub < 2, spread(left, 8), a2) + jnp.where(sub >= 6, b6, a6)
        far1 = far[:, 1] + jnp.where(sub < 2, a2, b2) + jnp.where(sub >= 6, spread(right, 6), b6)
        near = jnp.stack([near0, near1], axis=1)
        far = jnp.stack([far0, far1], axis=1)
        flat = cells.reshape(B * 16, depth)
        upper = flat.astype(jnp.bfloat16)
        lower = (flat - upper.astype(jnp.float32)).astype(jnp.bfloat16)
        along = jnp.dot(
            jnp.concatenate([upper, lower], axis=1), band[...],
            preferred_element_type=jnp.float32,
        ).reshape(B, 2, 8, depth)
        lap = along + 16.0 * near - far - 90.0 * cells
        here = pl.ds(TOP + base, B)
        if field == 1:
            shift = (RDEPTH - NSTEP + k + depth) % depth
            lap = lap + jnp.where(lane == RDEPTH, pltpu.roll(M[here], shift, 3), 0.0)
        value = 2.0 * cells - F[older, here] + C[here] * lap
        F[target, here] = value
        if field == 1:
            T[here] += value * F[NSTEP - k, here]

        @pl.when(k < NSTEP)
        def _():
            store_edges(k, c, value[:, 0], value[:, 1])
            send(field, k, c)

    def image_local(q):
        return pltpu.make_async_copy(
            T.at[pl.ds(TOP + q * B, B)], G.at[0, pl.ds(GROUP + q * B, B)], image_recv.at[0, q]
        )

    def image_copy(kind, q, source, target, device):
        return pltpu.make_async_remote_copy(
            src_ref=source,
            dst_ref=target,
            send_sem=image_send.at[kind, q],
            recv_sem=image_recv.at[kind, q],
            device_id=device,
            device_id_type=MESH,
        )

    def image_home(q):
        return image_copy(
            0, q, T.at[pl.ds(TOP + q * B, B)], G.at[0, pl.ds(GROUP + q * B, B)], twin
        )

    def image_across(q):
        span = pl.ds(GROUP + q * B, B)
        return image_copy(1, q, G.at[0, span], G.at[1, span], (across, me))

    def image_partner(q):
        span = pl.ds(GROUP + q * B, B)
        return image_copy(2, q, G.at[0, span], G.at[2, span], (partner, me))

    def image_onward(q):
        span = pl.ds(GROUP + q * B, B)
        return image_copy(3, q, G.at[1, span], G.at[3, span], (partner, me))

    @pl.when(jnp.logical_not(home))
    def _():
        over(chunks, lambda c: field_swap(0, c).start())

    for p in range(PIECES):
        model_across(p).start()
    over_slabs(lambda other: slab_copy(me, other).start())
    for p in range(PIECES):
        model_partner(p).start()
    own_packet.wait()
    over_slabs(lambda other: slab_copy(other, other).wait_recv())
    over_shots(lambda other: shot_copy(shot, other).start())
    for p in range(PIECES):
        model_across(p).wait_recv()
        model_onward(p).start()
        over(chunks // PIECES, lambda c: pack(0, p * (chunks // PIECES) + c))
    own_speed.wait()
    for p in range(PIECES):
        model_partner(p).wait_recv()
        model_onward(p).wait_recv()

    @pl.when(home)
    def _():
        def run(i):
            C[pl.ds(TOP + i * GROUP, GROUP)] = M[pl.ds(anchor + i * GROUP, GROUP)] * (1.0 / SCALE)

        over(rows // GROUP, run)

    @pl.when(jnp.logical_not(home))
    def _():
        def run(c):
            def fill(i):
                y = c * B + i * GROUP
                T[pl.ds(TOP + y, GROUP)] = M[pl.ds(anchor + y, GROUP)] * (1.0 / SCALE)

            over(B // GROUP, fill)
            speed_swap(c).start()
            field_swap(1, c).start()

        over(chunks, run)

    for p in range(PIECES):
        model_across(p).wait_send()
        model_partner(p).wait_send()
        model_onward(p).wait_send()

    def clear_drive(i):
        M[i] = zero_row

    over(TOP, clear_drive)

    def clear_drive_below(i):
        M[TOP + rows + i] = zero_row

    over(B, clear_drive_below)
    over_shots(lambda other: shot_copy(other, other).wait_recv())
    listed = shots * count * gathered.shape[2]
    samples = gathered[...].reshape(listed, depth)
    row = lax.broadcasted_iota(jnp.int32, (1, listed), 1)
    mine = (row % gathered.shape[2]) // CAP == shot
    place = jnp.where(mine, samples.T[NSTEP : NSTEP + 1].astype(jnp.int32), -1)
    cell = lax.broadcasted_iota(jnp.int32, (16 * 16, listed), 0)
    top_part = samples.astype(jnp.bfloat16)
    rest = samples - top_part.astype(jnp.float32)
    middle = rest.astype(jnp.bfloat16)
    low_part = (rest - middle.astype(jnp.float32)).astype(jnp.bfloat16)
    split = jnp.concatenate([top_part, middle, low_part], axis=1)

    def fill_drive(i):
        chosen = jnp.where(cell + i * 256 == place, 1.0, 0.0).astype(jnp.bfloat16)
        plane = jnp.dot(chosen, split, preferred_element_type=jnp.float32)
        plane = plane[:, :depth] + plane[:, depth : 2 * depth] + plane[:, 2 * depth :]
        M[pl.ds(TOP + i * 16, 16)] = (plane * SCALE).reshape(16, 2, 8, depth)

    over(rows // 16, fill_drive)

    def clear_total(c):
        T[pl.ds(TOP + c * B - SKEW, B)] = jnp.zeros((B, 2, 8, depth), jnp.float32)

    def during(low, value, high, act):
        @pl.when((value >= low) & (value < high))
        def _():
            act()

    def slot_work(t):
        @pl.when(jnp.logical_not(home))
        def _():
            def begin():
                field_swap(2, t).start()
                field_swap(3, t).start()

            during(0, t, chunks, begin)

        def source_step(i):
            k = NSTEP - i
            c = t - k + 1

            def act():
                @pl.when((k == 1) & (c < chunks))
                def _():
                    field_arrived(1, c)

                    @pl.when(jnp.logical_not(home))
                    def _():
                        speed_swap(c).wait_recv()

                advance(0, k, c)

            during(0, c, chunks + 1, act)

        over(NSTEP, source_step)
        late_t = t - DELAY

        @pl.when(late_t == 0)
        def _():
            @pl.when(jnp.logical_not(home))
            def _():
                over(chunks, lambda c: speed_swap(c).wait_send())

        def receiver_step(i):
            k = NSTEP - i
            c = late_t - k + 1

            def act():
                @pl.when(k == 1)
                def _():
                    clear_total(c)

                    @pl.when(c < chunks)
                    def _():
                        field_arrived(3, c)

                advance(1, k, c)

                @pl.when((k == NSTEP) & (c > 0))
                def _():
                    @pl.when(home)
                    def _():
                        image_local(c - 1).start()

                    @pl.when(jnp.logical_not(home))
                    def _():
                        image_home(c - 1).start()

            during(0, c, chunks + 1, act)

        over(NSTEP, receiver_step)
        during(0, late_t + 1, chunks, lambda: pack(1, late_t + 1))
        made = late_t - NSTEP - LAG_A

        def pass_on():
            @pl.when(home)
            def _():
                image_local(made).wait()

            @pl.when(jnp.logical_not(home))
            def _():
                image_home(made).wait_recv()

            image_across(made).start()
            image_partner(made).start()

        during(0, made, chunks, pass_on)
        reached = made - LAG_B

        def relay():
            image_across(reached).wait_recv()
            image_onward(reached).start()

        during(0, reached, chunks, relay)

    over(DELAY + NSTEP + chunks + LAG_A + LAG_B, slot_work)

    for q in range(chunks):
        image_partner(q).wait_recv()
        image_onward(q).wait_recv()

    owners = [shot, across, partner, beyond]

    def collect(i):
        y = i * GROUP
        result = jnp.zeros((GROUP, 2, 8, depth), jnp.float32)
        for s in range(4):
            first = jnp.clip(shot * block + y - anchors[owners[s]], -GROUP, rows) + GROUP
            result = result + G[s, pl.ds(first, GROUP)]
        out_ref[pl.ds(y, GROUP)] = result

    over(block // GROUP, collect)

    over_slabs(lambda other: slab_copy(me, other).wait_send())
    over_shots(lambda other: shot_copy(shot, other).wait_send())

    @pl.when(jnp.logical_not(home))
    def _():
        def run(c):
            for i in range(4):
                field_swap(i, c).wait_send()
            image_home(c).wait_send()

        over(chunks, run)

    def settle_image(q):
        image_across(q).wait_send()
        image_partner(q).wait_send()
        image_onward(q).wait_send()

    over(chunks, settle_image)
    over(chunks, lambda c: sent(1, 0, c))

    def settle_halo(k):
        over(chunks + 1, lambda c: sent(1, k + 1, c))

    over(NSTEP - 1, settle_halo)


def waves(anchors, now, prev, last, late, speed_model, packet):
    rows, _, _, depth = now.shape
    block = speed_model.shape[0]
    shots, slabs = lax.axis_size("shot"), lax.axis_size("slab")
    chunks = rows // B
    padded = TOP + rows + B
    anywhere = pl.BlockSpec(memory_space=pl.ANY)
    dma = pltpu.SemaphoreType.DMA
    edge_all = 2 * (rows + 2 * B)
    return pl.pallas_call(
        wave_kernel,
        out_shape=jax.ShapeDtypeStruct((block, 2, 8, depth), jnp.float32),
        in_specs=[pl.BlockSpec(memory_space=pltpu.SMEM)] + [anywhere] * 6,
        out_specs=pl.BlockSpec(memory_space=pltpu.VMEM),
        scratch_shapes=[
            pltpu.VMEM((NSTEP + 2, padded, 2, 8, depth), jnp.float32),
            pltpu.VMEM((NSTEP + 2, 2, edge_all, depth), jnp.float32),
            pltpu.VMEM((NSTEP, 2, edge_all, depth), jnp.float32),
            pltpu.VMEM((padded, 2, 8, depth), jnp.float32),
            pltpu.VMEM((padded, 2, 8, depth), jnp.float32),
            pltpu.VMEM((block * shots, 2, 8, depth), jnp.float32),
            pltpu.VMEM((4, rows + 2 * GROUP, 2, 8, depth), jnp.float32),
            pltpu.VMEM((2 * depth, depth), jnp.bfloat16),
            pltpu.VMEM((shots,) + packet.shape, jnp.float32),
            dma((2,)),
            dma((4, chunks)),
            dma((4, chunks)),
            dma((chunks,)),
            dma((chunks,)),
            dma((2, NSTEP, 2, chunks + 1)),
            dma((2, NSTEP, 2, chunks + 1)),
            dma((3, PIECES)),
            dma((3, PIECES)),
            dma((slabs,)),
            dma((slabs,)),
            dma((shots,)),
            dma((shots,)),
            dma((4, chunks)),
            dma((4, chunks)),
        ],
        compiler_params=pltpu.CompilerParams(
            collective_id=0, has_side_effects=True, vmem_limit_bytes=61 * 1024 * 1024
        ),
        name="waves",
    )(anchors, now, prev, last, late, speed_model, packet)


def per_device(fwd_prev, fwd_now, adj_late, adj_last, speed_model, anchors, traces, dest, rec_pos):
    def halves(array):
        return array.reshape(array.shape[-3], 2, 8, array.shape[-1])

    depth = fwd_now.shape[3]
    shots, slabs = lax.axis_size("shot"), lax.axis_size("slab")
    target = dest[:, 0]
    index = jnp.arange(target.shape[0], dtype=jnp.int32)
    ahead = (target[:, None] == target[None, :]) & (index[None, :] < index[:, None])
    rank = jnp.sum(ahead.astype(jnp.int32), axis=1)
    to_shot, to_slab = target // slabs, target % slabs
    device_shot = to_shot - to_shot % 2 + to_slab % 2
    device_slab = to_slab - to_slab % 2 + to_shot % 2
    slot = (device_slab * shots + device_shot) * CAP + rank
    listing = jnp.concatenate([traces, rec_pos.astype(jnp.float32)[None, :]], axis=0)
    wide = jnp.pad(listing.T, ((0, 0), (0, depth - NSTEP - 1)))
    packet = jnp.zeros((slabs * shots * CAP, depth), jnp.float32).at[slot].set(wide)
    packet = packet.reshape(slabs, shots * CAP, depth)
    image = waves(
        anchors, halves(fwd_now), halves(fwd_prev), halves(adj_last), halves(adj_late),
        halves(speed_model), packet,
    )
    return image.reshape(speed_model.shape)


def solution(mesh):
    placed = (
        P("shot", None, "slab", None),
        P("shot", None, "slab", None),
        P("shot", None, "slab", None),
        P("shot", None, "slab", None),
        P("shot", "slab", None),
        P(),
        P(None, ("shot", "slab")),
        P(("shot", "slab"), None),
        P(("shot", "slab")),
    )
    return jax.shard_map(
        per_device, mesh=mesh, in_specs=placed, out_specs=P("shot", "slab", None), check_vma=False
    )
```

```python
import jax
import jax.numpy as jnp
from jax import lax
from jax.experimental import pallas as pl
from jax.experimental.pallas import tpu as pltpu
from jax.sharding import PartitionSpec as P

NSTEP = 8
CAP = 2
RDEPTH = 3
B = 32
SKEW = B // NSTEP
TOP = B + SKEW
DELAY = 8
STRIDE = 1
PIECES = 4
GROUP = 8
LAG_A = 1
LAG_B = 1
WINDOW = 2
SCALE = 12.0

MESH = pl.DeviceIdType.MESH


def snap(n):
    late = (n + NSTEP - 1) // NSTEP
    return (n + 1) * (1 - late) + (n - 1) * late


def place_of(field, k):
    if field == 0:
        return snap(k)
    return NSTEP + (k + 1) % 2


def halo_slot(field, k):
    if field == 0:
        return k
    first = 1 - (k + NSTEP - 1) // NSTEP
    final = (k + 1) // NSTEP
    return k + NSTEP * first + 2 * final


def wave_kernel(
    anchors, traces, dest, rec_pos, now, prev, last, late, speed_in,
    out_ref,
    F, H, E, C, T, M, G, L, X, Y, band, packet, gathered,
    load_sem, field_send, field_recv, speed_send, speed_recv,
    halo_send, halo_recv, move_send, move_recv,
    slab_send, slab_recv, shot_send, shot_recv, image_send, image_recv,
):
    count = lax.axis_size("slab")
    shots = lax.axis_size("shot")
    shot = lax.axis_index("shot")
    me = lax.axis_index("slab")
    block = out_ref.shape[0]
    rows = now.shape[0]
    depth = now.shape[3]
    chunks = rows // B
    piece = block // PIECES
    edge_rows = 2 * B
    core = shot % 2
    side_of = me % 2
    home = core == side_of
    role_shot = shot - core + side_of
    role_slab = me - side_of + core
    twin = (role_shot, role_slab)
    partner = shot + 1 - 2 * core
    across = (shot + 2) % 4
    beyond = (partner + 2) % 4
    anchor = anchors[shot]
    left_device = (partner, me - 2 * (1 - core))
    right_device = (partner, me + 2 * core)
    has_left = role_slab > 0
    has_right = role_slab < count - 1
    sources = [now, prev, last, late]
    first_place = [place_of(0, 0), place_of(0, -1), place_of(1, 0), place_of(1, -1)]
    downward = shot // 2

    def chunk_at(c):
        return c * downward + (chunks - 1 - c) * (1 - downward)

    def base_of(k, c):
        y = c * B - SKEW * k
        return y * downward + (rows - B - y) * (1 - downward)

    zero_row = jnp.zeros((2, 8, depth), jnp.float32)
    zero_edge = jnp.zeros((8, depth), jnp.float32)

    def field_target(i, c):
        return F.at[first_place[i], pl.ds(TOP + chunk_at(c) * B, B)]

    def field_local(i, c):
        return pltpu.make_async_copy(
            sources[i].at[pl.ds(chunk_at(c) * B, B)], field_target(i, c), field_recv.at[i, c]
        )

    def field_swap(i, c):
        return pltpu.make_async_remote_copy(
            src_ref=sources[i].at[pl.ds(chunk_at(c) * B, B)],
            dst_ref=field_target(i, c),
            send_sem=field_send.at[i, c],
            recv_sem=field_recv.at[i, c],
            device_id=twin,
            device_id_type=MESH,
        )

    def field_arrived(i, c):
        @pl.when(home)
        def _():
            field_local(i, c).wait()

        @pl.when(jnp.logical_not(home))
        def _():
            field_swap(i, c).wait_recv()

    def over(n, act):
        def run(i, carry):
            act(i)
            return carry

        lax.fori_loop(0, n, run, 0)

    own_speed = pltpu.make_async_copy(speed_in, M.at[pl.ds(shot * block, block)], load_sem.at[0])
    own_packet = pltpu.make_async_copy(packet.at[me], gathered.at[shot, me], load_sem.at[1])
    own_speed.start()

    @pl.when(home)
    def _():
        for i in range(4):
            over(chunks, lambda c: field_local(i, c).start())

    barrier = pltpu.get_barrier_semaphore()

    def greet(device):
        pl.semaphore_signal(barrier, inc=1, device_id=device, device_id_type=MESH)

    def greet_slab(offset):
        greet((shot, (me + 1 + offset) % count))

    def greet_shot(offset):
        greet(((shot + 1 + offset) % shots, me))

    over(count - 1, greet_slab)
    over(shots - 1, greet_shot)

    pair = me // 2
    far_pair = pair + 2 * core - 1

    @pl.when(jnp.logical_not(home))
    def _():
        greet(twin)

    @pl.when((far_pair >= 0) & (far_pair < count // 2))
    def _():
        greet((partner, me + 2 * (2 * core - 1)))

    def clear_pads(i):
        for s in range(NSTEP + 2):
            F[s, i] = zero_row

    def clear_below(i):
        for s in range(NSTEP + 2):
            F[s, TOP + rows + i] = zero_row

    over(TOP, clear_pads)
    over(TOP, clear_below)

    def clear_speed(i):
        C[i] = zero_row

    over(TOP, clear_speed)

    def clear_speed_below(i):
        C[TOP + rows + i] = zero_row

    over(TOP, clear_speed_below)
    for s in range(2):
        L[s, 0:GROUP] = jnp.zeros((GROUP, 2, 8, depth), jnp.float32)
        L[s, GROUP + rows : 2 * GROUP + rows] = jnp.zeros((GROUP, 2, 8, depth), jnp.float32)

    def clear_span(s, side, y, lines):
        start = (B + y) * 2
        for g in range(2 * lines // 8):
            H[s, side, pl.ds(pl.multiple_of(start + 8 * g, 8), 8)] = zero_edge

    for s in range(NSTEP + 2):
        k = s if s < NSTEP else (0 if s == NSTEP else NSTEP - 1)
        outside = -SKEW * (k + 1) * downward + (rows + SKEW * k) * (1 - downward)
        after = rows * downward - B * (1 - downward)
        for side in range(2):
            clear_span(s, side, outside, SKEW)
            if k == 0:
                clear_span(s, side, after, B)

    def clear_halo(side):
        def run(i):
            for s in range(NSTEP + 2):
                H[s, side, pl.ds(i * 8, 8)] = zero_edge

        over(H.shape[2] // 8, run)

    @pl.when(jnp.logical_not(has_left))
    def _():
        clear_halo(0)

    @pl.when(jnp.logical_not(has_right))
    def _():
        clear_halo(1)

    line = lax.broadcasted_iota(jnp.int32, (2 * depth, depth), 0)
    column = lax.broadcasted_iota(jnp.int32, (2 * depth, depth), 1)
    apart = (line % depth) - column
    apart = apart * apart
    weight = jnp.where(apart == 1, 16.0, jnp.where(apart == 4, -1.0, 0.0))
    band[...] = weight.astype(jnp.bfloat16)

    listeners = dest.shape[1]
    goal = dest[...]
    first_index = lax.broadcasted_iota(jnp.int32, (listeners, listeners), 0)
    second_index = lax.broadcasted_iota(jnp.int32, (listeners, listeners), 1)
    spelled = goal.astype(jnp.float32)
    upright = jnp.sum(
        jnp.where(first_index == second_index, spelled, 0.0), axis=1, keepdims=True
    )
    ahead = jnp.where((upright == spelled) & (first_index < second_index), 1.0, 0.0)
    rank = jnp.sum(ahead, axis=0, keepdims=True).astype(jnp.int32)
    to_shot, to_slab = lax.div(goal, count), lax.rem(goal, count)
    holder_shot = to_shot - lax.rem(to_shot, 2) + lax.rem(to_slab, 2)
    holder_slab = to_slab - lax.rem(to_slab, 2) + lax.rem(to_shot, 2)
    slot_row = (holder_slab * shots + holder_shot) * CAP + rank
    slots = count * shots * CAP
    picked = jnp.where(
        lax.broadcasted_iota(jnp.int32, (slots, listeners), 0) == slot_row, 1.0, 0.0
    ).astype(jnp.bfloat16)
    listing = jnp.concatenate(
        [
            traces[...],
            rec_pos[...].astype(jnp.float32),
            jnp.zeros((depth - NSTEP - 1, listeners), jnp.float32),
        ],
        axis=0,
    )
    written = jnp.zeros((slots, depth), jnp.float32)
    for _ in range(3):
        part = listing.astype(jnp.bfloat16)
        listing = listing - part.astype(jnp.float32)
        written = written + lax.dot_general(
            picked, part, (((1,), (1,)), ((), ())), preferred_element_type=jnp.float32
        )
    packet[...] = written.reshape(count, shots * CAP, depth)
    own_packet.start()

    pl.semaphore_wait(
        barrier,
        count - 1 + shots - 1
        + jnp.where(home, 0, 1)
        + jnp.where((far_pair >= 0) & (far_pair < count // 2), 1, 0),
    )

    def slab_copy(source, target):
        return pltpu.make_async_remote_copy(
            src_ref=packet.at[target],
            dst_ref=gathered.at[shot, source],
            send_sem=slab_send.at[target],
            recv_sem=slab_recv.at[source],
            device_id=(shot, target),
            device_id_type=MESH,
        )

    def shot_copy(source, target):
        return pltpu.make_async_remote_copy(
            src_ref=gathered.at[source],
            dst_ref=gathered.at[source],
            send_sem=shot_send.at[target],
            recv_sem=shot_recv.at[source],
            device_id=(target, me),
            device_id_type=MESH,
        )

    def over_slabs(act):
        over(count - 1, lambda i: act((me + 1 + i) % count))

    def over_shots(act):
        over(shots - 1, lambda i: act((shot + 1 + i) % shots))

    def move(kind, p, source, target, device):
        return pltpu.make_async_remote_copy(
            src_ref=source,
            dst_ref=target,
            send_sem=move_send.at[kind, p],
            recv_sem=move_recv.at[kind, p],
            device_id=(device, me),
            device_id_type=MESH,
        )

    def model_across(p):
        span = M.at[pl.ds(shot * block + p * piece, piece)]
        return move(0, p, speed_in.at[pl.ds(p * piece, piece)], span, across)

    def model_partner(p):
        span = M.at[pl.ds(shot * block + p * piece, piece)]
        return move(1, p, speed_in.at[pl.ds(p * piece, piece)], span, partner)

    def model_onward(p):
        span = M.at[pl.ds(across * block + p * piece, piece)]
        return move(2, p, span, span, partner)

    def speed_swap(c):
        span = pl.ds(TOP + chunk_at(c) * B, B)
        return pltpu.make_async_remote_copy(
            src_ref=T.at[span],
            dst_ref=C.at[span],
            send_sem=speed_send.at[c],
            recv_sem=speed_recv.at[c],
            device_id=twin,
            device_id_type=MESH,
        )

    def transfer(field, k, side, c):
        span = pl.ds(pl.multiple_of((base_of(k, c) + B) * 2, 8), edge_rows)
        device = left_device if side == 0 else right_device
        return pltpu.make_async_remote_copy(
            src_ref=E.at[k, side, span],
            dst_ref=H.at[halo_slot(field, k), 1 - side, span],
            send_sem=halo_send.at[field, k, side, c],
            recv_sem=halo_recv.at[field, k, 1 - side, c],
            device_id=device,
            device_id_type=MESH,
        )

    def both_sides(act_left, act_right):
        @pl.when(has_left)
        def _():
            act_left()

        @pl.when(has_right)
        def _():
            act_right()

    def send(field, k, c):
        both_sides(
            lambda: transfer(field, k, 0, c).start(), lambda: transfer(field, k, 1, c).start()
        )

    def sent(field, k, c):
        both_sides(
            lambda: transfer(field, k, 0, c).wait_send(),
            lambda: transfer(field, k, 1, c).wait_send(),
        )

    def receive(field, k, c):
        both_sides(
            lambda: transfer(field, k, 1, c).wait_recv(),
            lambda: transfer(field, k, 0, c).wait_recv(),
        )

    quad = lax.broadcasted_iota(jnp.int32, (B // 4, 8, depth), 1)

    def store_edges(k, c, v0, v1):
        a = v0.reshape(B // 4, 4, 8, depth)
        b = v1.reshape(B // 4, 4, 8, depth)
        low, high = a[:, 0], pltpu.roll(b[:, 0], 2, 1)
        for i in range(1, 4):
            low = jnp.where(quad >= 2 * i, pltpu.roll(a[:, i], 2 * i, 1), low)
            turned = b[:, i] if i == 3 else pltpu.roll(b[:, i], 2 * i + 2, 1)
            high = jnp.where(quad >= 2 * i, turned, high)
        span = pl.ds(pl.multiple_of((base_of(k, c) + B) * 2, 8), edge_rows)
        E[k, 0, span] = low.reshape(edge_rows, depth)
        E[k, 1, span] = high.reshape(edge_rows, depth)

    def pack(field, c):
        field_arrived(2 * field, c)
        if field == 1:
            sent(0, 0, c)
        cells = F[first_place[2 * field], pl.ds(TOP + chunk_at(c) * B, B)]
        store_edges(0, c, cells[:, 0], cells[:, 1])
        send(field, 0, c)

    sub = lax.broadcasted_iota(jnp.int32, (B, 8, depth), 1)
    lane = lax.broadcasted_iota(jnp.int32, (B, 2, 8, depth), 3)

    def turned(ghost, shift):
        if shift % 8 == 0:
            return ghost
        return pltpu.roll(ghost, shift % 8, 1)

    def spread(ghost, shift):
        parts = [turned(ghost, shift - 2 * i) for i in range(4)]
        return jnp.stack(parts, axis=1).reshape(B, 8, depth)

    def advance(field, k, c):
        base = base_of(k, c)
        newer, older, target = place_of(field, k - 1), place_of(field, k - 2), place_of(field, k)

        @pl.when((k > 1) | (c < chunks))
        def _():
            receive(field, k - 1, c)

        if field == 1:
            @pl.when(k < NSTEP)
            def _():
                sent(0, k, c)

        window = F[newer, pl.ds(TOP + base - 2, B + 4)]
        cells = window[2 : B + 2]
        near = window[1 : B + 1] + window[3 : B + 3]
        far = window[0:B] + window[4 : B + 4]
        v0, v1 = cells[:, 0], cells[:, 1]
        span = pl.ds(pl.multiple_of((base + B) * 2, 8), edge_rows)
        slot = halo_slot(field, k - 1)
        left = H[slot, 0, span].reshape(B // 4, 8, depth)
        right = H[slot, 1, span].reshape(B // 4, 8, depth)
        a1, b1 = pltpu.roll(v0, 1, 1), pltpu.roll(v1, 1, 1)
        a2, b2 = pltpu.roll(v0, 2, 1), pltpu.roll(v1, 2, 1)
        a7, b7 = pltpu.roll(v0, 7, 1), pltpu.roll(v1, 7, 1)
        a6, b6 = pltpu.roll(v0, 6, 1), pltpu.roll(v1, 6, 1)
        near0 = near[:, 0] + jnp.where(sub < 1, spread(left, 7), a1) + jnp.where(sub >= 7, b7, a7)
        near1 = near[:, 1] + jnp.where(sub < 1, a1, b1) + jnp.where(sub >= 7, spread(right, 7), b7)
        far0 = far[:, 0] + jnp.where(sub < 2, spread(left, 8), a2) + jnp.where(sub >= 6, b6, a6)
        far1 = far[:, 1] + jnp.where(sub < 2, a2, b2) + jnp.where(sub >= 6, spread(right, 6), b6)
        near = jnp.stack([near0, near1], axis=1)
        far = jnp.stack([far0, far1], axis=1)
        flat = cells.reshape(B * 16, depth)
        upper = flat.astype(jnp.bfloat16)
        lower = (flat - upper.astype(jnp.float32)).astype(jnp.bfloat16)
        along = jnp.dot(
            jnp.concatenate([upper, lower], axis=1), band[...],
            preferred_element_type=jnp.float32,
        ).reshape(B, 2, 8, depth)
        lap = along + 16.0 * near - far - 90.0 * cells
        here = pl.ds(TOP + base, B)
        if field == 1:
            shift = (RDEPTH - NSTEP + k + depth) % depth
            lap = lap + jnp.where(lane == RDEPTH, pltpu.roll(M[here], shift, 3), 0.0)
        value = 2.0 * cells - F[older, here] + C[here] * lap
        F[target, here] = value
        if field == 1:
            T[here] += value * F[NSTEP - k, here]

        @pl.when(k < NSTEP)
        def _():
            store_edges(k, c, value[:, 0], value[:, 1])
            send(field, k, c)

    def image_rows(q):
        return T.at[pl.ds(TOP + chunk_at(q) * B, B)]

    def image_place(s, q):
        return G.at[s, pl.ds(chunk_at(q) * B, B)]

    def image_local(q):
        return pltpu.make_async_copy(image_rows(q), image_place(0, q), image_recv.at[0, q])

    def image_copy(kind, q, source, target, device):
        return pltpu.make_async_remote_copy(
            src_ref=source,
            dst_ref=target,
            send_sem=image_send.at[kind, q],
            recv_sem=image_recv.at[kind, q],
            device_id=device,
            device_id_type=MESH,
        )

    def image_home(q):
        return image_copy(0, q, image_rows(q), image_place(0, q), twin)

    def image_partner(q):
        return image_copy(1, q, image_place(0, q), image_place(1, q), (partner, me))

    def image_across(e):
        span = pl.ds(e * B, B)
        return image_copy(2, e, X.at[span], Y.at[span], (across, me))

    def share(owner, y):
        total = jnp.zeros((GROUP, 2, 8, depth), jnp.float32)
        for s, giver in ((0, shot), (1, partner)):
            first = jnp.clip(owner * block + y - anchors[giver], -GROUP, rows) + GROUP
            total = total + L[s, pl.ds(first, GROUP)]
        return total

    @pl.when(jnp.logical_not(home))
    def _():
        over(2 * WINDOW, lambda c: field_swap(0, c).start())

    for p in range(PIECES):
        model_across(p).start()

    over_slabs(lambda other: slab_copy(me, other).start())
    for p in range(PIECES):
        model_partner(p).start()
    own_packet.wait()
    over_slabs(lambda other: slab_copy(other, other).wait_recv())
    over_shots(lambda other: shot_copy(shot, other).start())

    def first_pack(c):
        pack(0, c)

        @pl.when(jnp.logical_not(home))
        def _():
            following = c + 2 * WINDOW

            @pl.when(following < chunks)
            def _():
                field_swap(0, following).start()

            @pl.when((following >= chunks) & (following < chunks + WINDOW))
            def _():
                field_swap(1, following - chunks).start()

    for p in range(PIECES):
        model_across(p).wait_recv()
        model_onward(p).start()
        over(chunks // PIECES, lambda c: first_pack(p * (chunks // PIECES) + c))
    own_speed.wait()
    for p in range(PIECES):
        model_partner(p).wait_recv()
        model_onward(p).wait_recv()

    @pl.when(home)
    def _():
        def run(i):
            C[pl.ds(TOP + i * GROUP, GROUP)] = M[pl.ds(anchor + i * GROUP, GROUP)] * (1.0 / SCALE)

        over(rows // GROUP, run)

    @pl.when(jnp.logical_not(home))
    def _():
        def run(c):
            def fill(i):
                y = chunk_at(c) * B + i * GROUP
                T[pl.ds(TOP + y, GROUP)] = M[pl.ds(anchor + y, GROUP)] * (1.0 / SCALE)

            over(B // GROUP, fill)

            @pl.when(c < WINDOW)
            def _():
                speed_swap(c).start()

        over(chunks, run)

    for p in range(PIECES):
        model_across(p).wait_send()
        model_partner(p).wait_send()
        model_onward(p).wait_send()

    def clear_drive(i):
        M[i] = zero_row

    over(TOP, clear_drive)

    def clear_drive_below(i):
        M[TOP + rows + i] = zero_row

    over(TOP, clear_drive_below)
    over_shots(lambda other: shot_copy(other, other).wait_recv())
    listed = shots * count * gathered.shape[2]
    samples = gathered[...].reshape(listed, depth)
    row = lax.broadcasted_iota(jnp.int32, (1, listed), 1)
    mine = (row % gathered.shape[2]) // CAP == shot
    place = jnp.where(mine, samples.T[NSTEP : NSTEP + 1].astype(jnp.int32), -1)
    cell = lax.broadcasted_iota(jnp.int32, (16 * 16, listed), 0)
    top_part = samples.astype(jnp.bfloat16)
    rest = samples - top_part.astype(jnp.float32)
    middle = rest.astype(jnp.bfloat16)
    low_part = (rest - middle.astype(jnp.float32)).astype(jnp.bfloat16)
    split = jnp.concatenate([top_part, middle, low_part], axis=1)

    def fill_drive(i):
        chosen = jnp.where(cell + i * 256 == place, 1.0, 0.0).astype(jnp.bfloat16)
        plane = jnp.dot(chosen, split, preferred_element_type=jnp.float32)
        plane = plane[:, :depth] + plane[:, depth : 2 * depth] + plane[:, 2 * depth :]
        M[pl.ds(TOP + i * 16, 16)] = (plane * SCALE).reshape(16, 2, 8, depth)

    over(rows // 16, fill_drive)

    def clear_total(c):
        T[pl.ds(TOP + base_of(1, c), B)] = jnp.zeros((B, 2, 8, depth), jnp.float32)

    def during(low, value, high, act):
        @pl.when((value >= low) & (value < high))
        def _():
            act()

    def slot_work(t):
        def source_step(i):
            k = NSTEP - i
            c = t - k + 1

            def act():
                @pl.when((k == 1) & (c < chunks))
                def _():
                    field_arrived(1, c)

                    @pl.when(jnp.logical_not(home))
                    def _():
                        speed_swap(c).wait_recv()

                        @pl.when(c + WINDOW < chunks)
                        def _():
                            speed_swap(c + WINDOW).start()
                            field_swap(1, c + WINDOW).start()

                        @pl.when(c + WINDOW >= chunks)
                        def _():
                            field_swap(2, c + WINDOW - chunks).start()
                            field_swap(3, c + WINDOW - chunks).start()

                advance(0, k, c)

            during(0, c, chunks + 1, act)

        over(NSTEP, source_step)
        late_t = t - DELAY

        @pl.when(late_t == 0)
        def _():
            @pl.when(jnp.logical_not(home))
            def _():
                over(chunks, lambda c: speed_swap(c).wait_send())

        def receiver_step(i):
            k = NSTEP - STRIDE * i - (late_t + 1) % STRIDE
            c = (late_t - k + 1) // STRIDE

            def act():
                @pl.when(k == 1)
                def _():
                    clear_total(c)

                    @pl.when(c < chunks)
                    def _():
                        field_arrived(3, c)

                        @pl.when(jnp.logical_not(home) & (c + WINDOW < chunks))
                        def _():
                            field_swap(2, c + WINDOW).start()
                            field_swap(3, c + WINDOW).start()

                advance(1, k, c)

                @pl.when((k == NSTEP) & (c > 0))
                def _():
                    @pl.when(home)
                    def _():
                        image_local(c - 1).start()

                    @pl.when(jnp.logical_not(home))
                    def _():
                        image_home(c - 1).start()

            during(0, c, chunks + 1, act)

        over(NSTEP // STRIDE, receiver_step)

        @pl.when((late_t + 1) % STRIDE == 0)
        def _():
            following = (late_t + 1) // STRIDE
            during(0, following, chunks, lambda: pack(1, following))


        def pass_on(q):
            @pl.when(home)
            def _():
                image_local(q).wait()

            @pl.when(jnp.logical_not(home))
            def _():
                image_home(q).wait_recv()

            image_partner(q).start()
            y = chunk_at(q) * B
            L[0, pl.ds(GROUP + y, B)] = G[0, pl.ds(y, B)]

        def relay(q):
            image_partner(q).wait_recv()
            y = chunk_at(q) * B
            L[1, pl.ds(GROUP + y, B)] = G[1, pl.ds(y, B)]
            per_block = block // B
            e = chunk_at(q) % per_block

            @pl.when(chunk_at(q) // per_block == core)
            def _():
                for g in range(B // GROUP):
                    X[pl.ds(e * B + g * GROUP, GROUP)] = share(across, e * B + g * GROUP)
                image_across(e).start()

        def every(v, act):
            @pl.when(v % STRIDE == 0)
            def _():
                during(0, v // STRIDE, chunks, lambda: act(v // STRIDE))

        made = late_t - (NSTEP - 1) - STRIDE - LAG_A
        every(made, pass_on)
        every(made - LAG_B, relay)

    over(DELAY + NSTEP + STRIDE * chunks + LAG_A + LAG_B, slot_work)

    def collect(e):
        image_across(e).wait_recv()
        for g in range(B // GROUP):
            y = e * B + g * GROUP
            out_ref[pl.ds(y, GROUP)] = share(shot, y) + Y[pl.ds(y, GROUP)]

    over(block // B, collect)

    over_slabs(lambda other: slab_copy(me, other).wait_send())
    over_shots(lambda other: shot_copy(shot, other).wait_send())

    @pl.when(jnp.logical_not(home))
    def _():
        def run(c):
            for i in range(4):
                field_swap(i, c).wait_send()
            image_home(c).wait_send()

        over(chunks, run)

    def settle_image(q):
        image_partner(q).wait_send()

    over(chunks, settle_image)
    over(block // B, lambda e: image_across(e).wait_send())
    over(chunks, lambda c: sent(1, 0, c))

    def settle_halo(k):
        over(chunks + 1, lambda c: sent(1, k + 1, c))

    over(NSTEP - 1, settle_halo)


def waves(anchors, traces, dest, rec_pos, now, prev, last, late, speed_model):
    rows, _, _, depth = now.shape
    block = speed_model.shape[0]
    shots, slabs = lax.axis_size("shot"), lax.axis_size("slab")
    chunks = rows // B
    padded = TOP + rows + TOP
    anywhere = pl.BlockSpec(memory_space=pl.ANY)
    dma = pltpu.SemaphoreType.DMA
    edge_all = 2 * (rows + 2 * B)
    return pl.pallas_call(
        wave_kernel,
        out_shape=jax.ShapeDtypeStruct((block, 2, 8, depth), jnp.float32),
        in_specs=[pl.BlockSpec(memory_space=pltpu.SMEM)]
        + [pl.BlockSpec(memory_space=pltpu.VMEM)] * 3
        + [anywhere] * 5,
        out_specs=pl.BlockSpec(memory_space=pltpu.VMEM),
        scratch_shapes=[
            pltpu.VMEM((NSTEP + 2, padded, 2, 8, depth), jnp.float32),
            pltpu.VMEM((NSTEP + 2, 2, edge_all, depth), jnp.float32),
            pltpu.VMEM((NSTEP, 2, edge_all, depth), jnp.float32),
            pltpu.VMEM((padded, 2, 8, depth), jnp.float32),
            pltpu.VMEM((padded, 2, 8, depth), jnp.float32),
            pltpu.VMEM((block * shots, 2, 8, depth), jnp.float32),
            pltpu.VMEM((2, rows, 2, 8, depth), jnp.float32),
            pltpu.VMEM((2, rows + 2 * GROUP, 2, 8, depth), jnp.float32),
            pltpu.VMEM((block, 2, 8, depth), jnp.float32),
            pltpu.VMEM((block, 2, 8, depth), jnp.float32),
            pltpu.VMEM((2 * depth, depth), jnp.bfloat16),
            pltpu.VMEM((slabs, shots * CAP, depth), jnp.float32),
            pltpu.VMEM((shots, slabs, shots * CAP, depth), jnp.float32),
            dma((2,)),
            dma((4, chunks)),
            dma((4, chunks)),
            dma((chunks,)),
            dma((chunks,)),
            dma((2, NSTEP, 2, chunks + 1)),
            dma((2, NSTEP, 2, chunks + 1)),
            dma((3, PIECES)),
            dma((3, PIECES)),
            dma((slabs,)),
            dma((slabs,)),
            dma((shots,)),
            dma((shots,)),
            dma((3, chunks)),
            dma((3, chunks)),
        ],
        compiler_params=pltpu.CompilerParams(
            collective_id=0, has_side_effects=True, vmem_limit_bytes=61 * 1024 * 1024
        ),
        name="waves",
    )(anchors, traces, dest, rec_pos, now, prev, last, late, speed_model)


def per_device(fwd_prev, fwd_now, adj_late, adj_last, speed_model, anchors, traces, dest, rec_pos):
    def halves(array):
        return array.reshape(array.shape[-3], 2, 8, array.shape[-1])

    image = waves(
        anchors, traces, dest.reshape(1, -1), rec_pos.reshape(1, -1),
        halves(fwd_now), halves(fwd_prev), halves(adj_last), halves(adj_late),
        halves(speed_model),
    )
    return image.reshape(speed_model.shape)


def solution(mesh):
    placed = (
        P("shot", None, "slab", None),
        P("shot", None, "slab", None),
        P("shot", None, "slab", None),
        P("shot", None, "slab", None),
        P("shot", "slab", None),
        P(),
        P(None, ("shot", "slab")),
        P(("shot", "slab"), None),
        P(("shot", "slab")),
    )
    return jax.shard_map(
        per_device, mesh=mesh, in_specs=placed, out_specs=P("shot", "slab", None), check_vma=False
    )
```

```python
import jax
import jax.numpy as jnp
from jax import lax
from jax.experimental import pallas as pl
from jax.experimental.pallas import tpu as pltpu
from jax.sharding import PartitionSpec as P

NSTEP = 8
CAP = 2
RDEPTH = 3
B = 32
SKEW = B // NSTEP
TOP = B + SKEW
DELAY = 8
STRIDE = 1
PIECES = 4
GROUP = 8
EARLY = 6
LAG_A = 1
LAG_B = 1
WINDOW = 2
SCALE = 12.0

MESH = pl.DeviceIdType.MESH


def snap(n):
    late = (n + NSTEP - 1) // NSTEP
    return (n + 1) * (1 - late) + (n - 1) * late


def place_of(field, k):
    if field == 0:
        return snap(k)
    return NSTEP + (k + 1) % 2


def halo_slot(field, k):
    if field == 0:
        return k
    first = 1 - (k + NSTEP - 1) // NSTEP
    final = (k + 1) // NSTEP
    return k + NSTEP * first + 2 * final


def wave_kernel(
    anchors, traces, dest, rec_pos, now, prev, last, late, speed_in,
    out_ref,
    F, H, E, C, T, M, G, L, X, Y, band, packet, gathered,
    load_sem, field_send, field_recv, speed_send, speed_recv,
    halo_send, halo_recv, move_send, move_recv,
    slab_send, slab_recv, shot_send, shot_recv, image_send, image_recv,
):
    count = lax.axis_size("slab")
    shots = lax.axis_size("shot")
    shot = lax.axis_index("shot")
    me = lax.axis_index("slab")
    block = out_ref.shape[0]
    rows = now.shape[0]
    depth = now.shape[3]
    chunks = rows // B
    piece = block // PIECES
    edge_rows = 2 * B
    core = shot % 2
    side_of = me % 2
    home = core == side_of
    role_shot = shot - core + side_of
    role_slab = me - side_of + core
    twin = (role_shot, role_slab)
    partner = shot + 1 - 2 * core
    across = (shot + 2) % 4
    beyond = (partner + 2) % 4
    anchor = anchors[shot]
    left_device = (partner, me - 2 * (1 - core))
    right_device = (partner, me + 2 * core)
    has_left = role_slab > 0
    has_right = role_slab < count - 1
    sources = [now, prev, last, late]
    first_place = [place_of(0, 0), place_of(0, -1), place_of(1, 0), place_of(1, -1)]
    downward = shot // 2

    def chunk_at(c):
        return c * downward + (chunks - 1 - c) * (1 - downward)

    def base_of(k, c):
        y = c * B - SKEW * k
        return y * downward + (rows - B - y) * (1 - downward)

    zero_row = jnp.zeros((2, 8, depth), jnp.float32)
    zero_edge = jnp.zeros((8, depth), jnp.float32)

    def field_target(i, c):
        return F.at[first_place[i], pl.ds(TOP + chunk_at(c) * B, B)]

    def field_local(i, c):
        return pltpu.make_async_copy(
            sources[i].at[pl.ds(chunk_at(c) * B, B)], field_target(i, c), field_recv.at[i, c]
        )

    def field_swap(i, c):
        return pltpu.make_async_remote_copy(
            src_ref=sources[i].at[pl.ds(chunk_at(c) * B, B)],
            dst_ref=field_target(i, c),
            send_sem=field_send.at[i, c],
            recv_sem=field_recv.at[i, c],
            device_id=twin,
            device_id_type=MESH,
        )

    def field_arrived(i, c):
        @pl.when(home)
        def _():
            field_local(i, c).wait()

        @pl.when(jnp.logical_not(home))
        def _():
            field_swap(i, c).wait_recv()

    def over(n, act):
        def run(i, carry):
            act(i)
            return carry

        lax.fori_loop(0, n, run, 0)

    own_speed = pltpu.make_async_copy(speed_in, M.at[pl.ds(shot * block, block)], load_sem.at[0])
    own_packet = pltpu.make_async_copy(packet.at[me], gathered.at[shot, me], load_sem.at[1])
    own_speed.start()

    @pl.when(home)
    def _():
        for i in range(4):
            over(chunks, lambda c: field_local(i, c).start())

    barrier = pltpu.get_barrier_semaphore()

    def greet(device):
        pl.semaphore_signal(barrier, inc=1, device_id=device, device_id_type=MESH)

    def greet_slab(offset):
        greet((shot, (me + 1 + offset) % count))

    def greet_shot(offset):
        greet(((shot + 1 + offset) % shots, me))

    over(count - 1, greet_slab)
    over(shots - 1, greet_shot)

    pair = me // 2
    far_pair = pair + 2 * core - 1

    @pl.when(jnp.logical_not(home))
    def _():
        greet(twin)

    @pl.when((far_pair >= 0) & (far_pair < count // 2))
    def _():
        greet((partner, me + 2 * (2 * core - 1)))

    pl.semaphore_wait(
        barrier,
        count - 1 + shots - 1
        + jnp.where(home, 0, 1)
        + jnp.where((far_pair >= 0) & (far_pair < count // 2), 1, 0),
    )

    def slab_copy(source, target):
        return pltpu.make_async_remote_copy(
            src_ref=packet.at[target],
            dst_ref=gathered.at[shot, source],
            send_sem=slab_send.at[target],
            recv_sem=slab_recv.at[source],
            device_id=(shot, target),
            device_id_type=MESH,
        )

    def shot_copy(source, target):
        return pltpu.make_async_remote_copy(
            src_ref=gathered.at[source],
            dst_ref=gathered.at[source],
            send_sem=shot_send.at[target],
            recv_sem=shot_recv.at[source],
            device_id=(target, me),
            device_id_type=MESH,
        )

    def over_slabs(act):
        over(count - 1, lambda i: act((me + 1 + i) % count))

    def over_shots(act):
        over(shots - 1, lambda i: act((shot + 1 + i) % shots))

    def move(kind, p, source, target, device):
        return pltpu.make_async_remote_copy(
            src_ref=source,
            dst_ref=target,
            send_sem=move_send.at[kind, p],
            recv_sem=move_recv.at[kind, p],
            device_id=(device, me),
            device_id_type=MESH,
        )

    def model_across(p):
        span = M.at[pl.ds(shot * block + p * piece, piece)]
        return move(0, p, speed_in.at[pl.ds(p * piece, piece)], span, across)

    def model_partner(p):
        span = M.at[pl.ds(shot * block + p * piece, piece)]
        return move(1, p, speed_in.at[pl.ds(p * piece, piece)], span, partner)

    def model_onward(p):
        span = M.at[pl.ds(across * block + p * piece, piece)]
        return move(2, p, span, span, partner)

    def speed_swap(c):
        span = pl.ds(TOP + chunk_at(c) * B, B)
        return pltpu.make_async_remote_copy(
            src_ref=T.at[span],
            dst_ref=C.at[span],
            send_sem=speed_send.at[c],
            recv_sem=speed_recv.at[c],
            device_id=twin,
            device_id_type=MESH,
        )

    def transfer(field, k, side, c):
        span = pl.ds(pl.multiple_of((base_of(k, c) + B) * 2, 8), edge_rows)
        device = left_device if side == 0 else right_device
        return pltpu.make_async_remote_copy(
            src_ref=E.at[k, side, span],
            dst_ref=H.at[halo_slot(field, k), 1 - side, span],
            send_sem=halo_send.at[field, k, side, c],
            recv_sem=halo_recv.at[field, k, 1 - side, c],
            device_id=device,
            device_id_type=MESH,
        )

    def both_sides(act_left, act_right):
        @pl.when(has_left)
        def _():
            act_left()

        @pl.when(has_right)
        def _():
            act_right()

    def send(field, k, c):
        both_sides(
            lambda: transfer(field, k, 0, c).start(), lambda: transfer(field, k, 1, c).start()
        )

    def sent(field, k, c):
        both_sides(
            lambda: transfer(field, k, 0, c).wait_send(),
            lambda: transfer(field, k, 1, c).wait_send(),
        )

    def receive(field, k, c):
        both_sides(
            lambda: transfer(field, k, 1, c).wait_recv(),
            lambda: transfer(field, k, 0, c).wait_recv(),
        )

    quad = lax.broadcasted_iota(jnp.int32, (B // 4, 8, depth), 1)

    def store_edges(k, c, v0, v1):
        a = v0.reshape(B // 4, 4, 8, depth)
        b = v1.reshape(B // 4, 4, 8, depth)
        low, high = a[:, 0], pltpu.roll(b[:, 0], 2, 1)
        for i in range(1, 4):
            low = jnp.where(quad >= 2 * i, pltpu.roll(a[:, i], 2 * i, 1), low)
            turned = b[:, i] if i == 3 else pltpu.roll(b[:, i], 2 * i + 2, 1)
            high = jnp.where(quad >= 2 * i, turned, high)
        span = pl.ds(pl.multiple_of((base_of(k, c) + B) * 2, 8), edge_rows)
        E[k, 0, span] = low.reshape(edge_rows, depth)
        E[k, 1, span] = high.reshape(edge_rows, depth)

    def pack(field, c):
        field_arrived(2 * field, c)
        if field == 1:
            sent(0, 0, c)
        cells = F[first_place[2 * field], pl.ds(TOP + chunk_at(c) * B, B)]
        store_edges(0, c, cells[:, 0], cells[:, 1])
        send(field, 0, c)

    sub = lax.broadcasted_iota(jnp.int32, (B, 8, depth), 1)
    lane = lax.broadcasted_iota(jnp.int32, (B, 2, 8, depth), 3)

    def turned(ghost, shift):
        if shift % 8 == 0:
            return ghost
        return pltpu.roll(ghost, shift % 8, 1)

    def spread(ghost, shift):
        parts = [turned(ghost, shift - 2 * i) for i in range(4)]
        return jnp.stack(parts, axis=1).reshape(B, 8, depth)

    def advance(field, k, c):
        base = base_of(k, c)
        newer, older, target = place_of(field, k - 1), place_of(field, k - 2), place_of(field, k)

        @pl.when((k > 1) | (c < chunks))
        def _():
            receive(field, k - 1, c)

        if field == 1:
            @pl.when(k < NSTEP)
            def _():
                sent(0, k, c)

        window = F[newer, pl.ds(TOP + base - 2, B + 4)]
        cells = window[2 : B + 2]
        near = window[1 : B + 1] + window[3 : B + 3]
        far = window[0:B] + window[4 : B + 4]
        v0, v1 = cells[:, 0], cells[:, 1]
        span = pl.ds(pl.multiple_of((base + B) * 2, 8), edge_rows)
        slot = halo_slot(field, k - 1)
        left = H[slot, 0, span].reshape(B // 4, 8, depth)
        right = H[slot, 1, span].reshape(B // 4, 8, depth)
        a1, b1 = pltpu.roll(v0, 1, 1), pltpu.roll(v1, 1, 1)
        a2, b2 = pltpu.roll(v0, 2, 1), pltpu.roll(v1, 2, 1)
        a7, b7 = pltpu.roll(v0, 7, 1), pltpu.roll(v1, 7, 1)
        a6, b6 = pltpu.roll(v0, 6, 1), pltpu.roll(v1, 6, 1)
        near0 = near[:, 0] + jnp.where(sub < 1, spread(left, 7), a1) + jnp.where(sub >= 7, b7, a7)
        near1 = near[:, 1] + jnp.where(sub < 1, a1, b1) + jnp.where(sub >= 7, spread(right, 7), b7)
        far0 = far[:, 0] + jnp.where(sub < 2, spread(left, 8), a2) + jnp.where(sub >= 6, b6, a6)
        far1 = far[:, 1] + jnp.where(sub < 2, a2, b2) + jnp.where(sub >= 6, spread(right, 6), b6)
        near = jnp.stack([near0, near1], axis=1)
        far = jnp.stack([far0, far1], axis=1)
        flat = cells.reshape(B * 16, depth)
        upper = flat.astype(jnp.bfloat16)
        lower = (flat - upper.astype(jnp.float32)).astype(jnp.bfloat16)
        along = jnp.dot(
            jnp.concatenate([upper, lower], axis=1), band[...],
            preferred_element_type=jnp.float32,
        ).reshape(B, 2, 8, depth)
        lap = along + 16.0 * near - far - 90.0 * cells
        here = pl.ds(TOP + base, B)
        if field == 1:
            shift = (RDEPTH - NSTEP + k + depth) % depth
            lap = lap + jnp.where(lane == RDEPTH, pltpu.roll(M[here], shift, 3), 0.0)
        value = 2.0 * cells - F[older, here] + C[here] * lap
        F[target, here] = value
        if field == 1:
            T[here] += value * F[NSTEP - k, here]

        @pl.when(k < NSTEP)
        def _():
            store_edges(k, c, value[:, 0], value[:, 1])
            send(field, k, c)

    def step(field, k, c):
        empty = (k == NSTEP) & (c == 0)

        @pl.when(empty)
        def _():
            receive(field, k - 1, c)

        @pl.when(jnp.logical_not(empty))
        def _():
            advance(field, k, c)

    def image_rows(q):
        return T.at[pl.ds(TOP + chunk_at(q) * B, B)]

    def image_place(s, q):
        return G.at[s, pl.ds(chunk_at(q) * B, B)]

    def image_local(q):
        return pltpu.make_async_copy(image_rows(q), image_place(0, q), image_recv.at[0, q])

    def image_copy(kind, q, source, target, device):
        return pltpu.make_async_remote_copy(
            src_ref=source,
            dst_ref=target,
            send_sem=image_send.at[kind, q],
            recv_sem=image_recv.at[kind, q],
            device_id=device,
            device_id_type=MESH,
        )

    def image_home(q):
        return image_copy(0, q, image_rows(q), image_place(0, q), twin)

    def image_partner(q):
        return image_copy(1, q, image_place(0, q), image_place(1, q), (partner, me))

    def image_across(e):
        span = pl.ds(e * B, B)
        return image_copy(2, e, X.at[span], Y.at[span], (across, me))

    def share(owner, y):
        total = jnp.zeros((GROUP, 2, 8, depth), jnp.float32)
        for s, giver in ((0, shot), (1, partner)):
            first = jnp.clip(owner * block + y - anchors[giver], -GROUP, rows) + GROUP
            total = total + L[s, pl.ds(first, GROUP)]
        return total

    @pl.when(jnp.logical_not(home))
    def _():
        over(2 * WINDOW, lambda c: field_swap(0, c).start())

    for p in range(PIECES):
        model_across(p).start()

    for p in range(PIECES):
        model_partner(p).start()

    def clear_pads(i):
        for s in range(NSTEP + 2):
            F[s, i] = zero_row

    def clear_below(i):
        for s in range(NSTEP + 2):
            F[s, TOP + rows + i] = zero_row

    over(TOP, clear_pads)
    over(TOP, clear_below)

    def clear_speed(i):
        C[i] = zero_row

    over(TOP, clear_speed)

    def clear_speed_below(i):
        C[TOP + rows + i] = zero_row

    over(TOP, clear_speed_below)
    for s in range(2):
        L[s, 0:GROUP] = jnp.zeros((GROUP, 2, 8, depth), jnp.float32)
        L[s, GROUP + rows : 2 * GROUP + rows] = jnp.zeros((GROUP, 2, 8, depth), jnp.float32)

    def clear_span(s, side, y, lines):
        start = (B + y) * 2
        for g in range(2 * lines // 8):
            H[s, side, pl.ds(pl.multiple_of(start + 8 * g, 8), 8)] = zero_edge

    for s in range(NSTEP + 2):
        k = s if s < NSTEP else (0 if s == NSTEP else NSTEP - 1)
        outside = -SKEW * (k + 1) * downward + (rows + SKEW * k) * (1 - downward)
        after = rows * downward - B * (1 - downward)
        for side in range(2):
            clear_span(s, side, outside, SKEW)
            if k == 0:
                clear_span(s, side, after, B)

    def clear_halo(side):
        def run(i):
            for s in range(NSTEP + 2):
                H[s, side, pl.ds(i * 8, 8)] = zero_edge

        over(H.shape[2] // 8, run)

    @pl.when(jnp.logical_not(has_left))
    def _():
        clear_halo(0)

    @pl.when(jnp.logical_not(has_right))
    def _():
        clear_halo(1)

    line = lax.broadcasted_iota(jnp.int32, (2 * depth, depth), 0)
    column = lax.broadcasted_iota(jnp.int32, (2 * depth, depth), 1)
    apart = (line % depth) - column
    apart = apart * apart
    weight = jnp.where(apart == 1, 16.0, jnp.where(apart == 4, -1.0, 0.0))
    band[...] = weight.astype(jnp.bfloat16)

    listeners = dest.shape[1]
    goal = dest[...]
    first_index = lax.broadcasted_iota(jnp.int32, (listeners, listeners), 0)
    second_index = lax.broadcasted_iota(jnp.int32, (listeners, listeners), 1)
    spelled = goal.astype(jnp.float32)
    upright = jnp.sum(
        jnp.where(first_index == second_index, spelled, 0.0), axis=1, keepdims=True
    )
    ahead = jnp.where((upright == spelled) & (first_index < second_index), 1.0, 0.0)
    rank = jnp.sum(ahead, axis=0, keepdims=True).astype(jnp.int32)
    to_shot, to_slab = lax.div(goal, count), lax.rem(goal, count)
    holder_shot = to_shot - lax.rem(to_shot, 2) + lax.rem(to_slab, 2)
    holder_slab = to_slab - lax.rem(to_slab, 2) + lax.rem(to_shot, 2)
    slot_row = (holder_slab * shots + holder_shot) * CAP + rank
    slots = count * shots * CAP
    picked = jnp.where(
        lax.broadcasted_iota(jnp.int32, (slots, listeners), 0) == slot_row, 1.0, 0.0
    ).astype(jnp.bfloat16)
    listing = jnp.concatenate(
        [
            traces[...],
            rec_pos[...].astype(jnp.float32),
            jnp.zeros((depth - NSTEP - 1, listeners), jnp.float32),
        ],
        axis=0,
    )
    written = jnp.zeros((slots, depth), jnp.float32)
    for _ in range(3):
        part = listing.astype(jnp.bfloat16)
        listing = listing - part.astype(jnp.float32)
        written = written + lax.dot_general(
            picked, part, (((1,), (1,)), ((), ())), preferred_element_type=jnp.float32
        )
    packet[...] = written.reshape(count, shots * CAP, depth)
    own_packet.start()

    over_slabs(lambda other: slab_copy(me, other).start())
    own_packet.wait()
    over_slabs(lambda other: slab_copy(other, other).wait_recv())
    over_shots(lambda other: shot_copy(shot, other).start())

    def first_pack(c):
        pack(0, c)

        @pl.when(jnp.logical_not(home))
        def _():
            following = c + 2 * WINDOW

            @pl.when(following < chunks)
            def _():
                field_swap(0, following).start()

            @pl.when((following >= chunks) & (following < chunks + WINDOW))
            def _():
                field_swap(1, following - chunks).start()

    for p in range(PIECES):
        model_across(p).wait_recv()
        model_onward(p).start()
        over(chunks // PIECES, lambda c: first_pack(p * (chunks // PIECES) + c))
    own_speed.wait()
    for p in range(PIECES):
        model_partner(p).wait_recv()
        model_onward(p).wait_recv()

    @pl.when(home)
    def _():
        def run(i):
            C[pl.ds(TOP + i * GROUP, GROUP)] = M[pl.ds(anchor + i * GROUP, GROUP)] * (1.0 / SCALE)

        over(rows // GROUP, run)

    @pl.when(jnp.logical_not(home))
    def _():
        def run(c):
            def fill(i):
                y = chunk_at(c) * B + i * GROUP
                T[pl.ds(TOP + y, GROUP)] = M[pl.ds(anchor + y, GROUP)] * (1.0 / SCALE)

            over(B // GROUP, fill)

            @pl.when(c < WINDOW)
            def _():
                speed_swap(c).start()

        over(chunks, run)

    for p in range(PIECES):
        model_across(p).wait_send()
        model_partner(p).wait_send()
        model_onward(p).wait_send()

    def clear_drive(i):
        M[i] = zero_row

    over(TOP, clear_drive)

    def clear_drive_below(i):
        M[TOP + rows + i] = zero_row

    over(TOP, clear_drive_below)
    over_shots(lambda other: shot_copy(other, other).wait_recv())
    listed = shots * count * gathered.shape[2]
    samples = gathered[...].reshape(listed, depth)
    row = lax.broadcasted_iota(jnp.int32, (1, listed), 1)
    mine = (row % gathered.shape[2]) // CAP == shot
    place = jnp.where(mine, samples.T[NSTEP : NSTEP + 1].astype(jnp.int32), -1)
    cell = lax.broadcasted_iota(jnp.int32, (16 * 16, listed), 0)
    top_part = samples.astype(jnp.bfloat16)
    rest = samples - top_part.astype(jnp.float32)
    middle = rest.astype(jnp.bfloat16)
    low_part = (rest - middle.astype(jnp.float32)).astype(jnp.bfloat16)
    split = jnp.concatenate([top_part, middle, low_part], axis=1)

    def fill_drive(i):
        chosen = jnp.where(cell + i * 256 == place, 1.0, 0.0).astype(jnp.bfloat16)
        plane = jnp.dot(chosen, split, preferred_element_type=jnp.float32)
        plane = plane[:, :depth] + plane[:, depth : 2 * depth] + plane[:, 2 * depth :]
        M[pl.ds(TOP + i * 16, 16)] = (plane * SCALE).reshape(16, 2, 8, depth)

    over(rows // 16, fill_drive)

    def clear_total(c):
        T[pl.ds(TOP + base_of(1, c), B)] = jnp.zeros((B, 2, 8, depth), jnp.float32)

    def during(low, value, high, act):
        @pl.when((value >= low) & (value < high))
        def _():
            act()

    def settle():
        over_slabs(lambda other: slab_copy(me, other).wait_send())
        over_shots(lambda other: shot_copy(shot, other).wait_send())

        @pl.when(jnp.logical_not(home))
        def _():
            def run(c):
                for i in range(4):
                    field_swap(i, c).wait_send()

            over(chunks, run)
            over(chunks - 1, lambda c: image_home(c).wait_send())

        over(chunks - 1, lambda q: image_partner(q).wait_send())
        over(chunks, lambda c: sent(1, 0, c))

        def settle_halo(k):
            over(chunks + 1, lambda c: sent(1, k + 1, c))

        over(NSTEP - 1, settle_halo)

    def slot_work(t):
        @pl.when(t == DELAY + NSTEP + STRIDE * chunks)
        def _():
            settle()

        def source_step(i):
            k = NSTEP - i
            c = t - k + 1

            def act():
                @pl.when((k == 1) & (c < chunks))
                def _():
                    field_arrived(1, c)

                    @pl.when(jnp.logical_not(home))
                    def _():
                        speed_swap(c).wait_recv()

                        @pl.when(c + WINDOW < chunks)
                        def _():
                            speed_swap(c + WINDOW).start()
                            field_swap(1, c + WINDOW).start()

                        @pl.when(c + WINDOW >= chunks)
                        def _():
                            field_swap(2, c + WINDOW - chunks).start()
                            field_swap(3, c + WINDOW - chunks).start()

                step(0, k, c)

            during(0, c, chunks + 1, act)

        late_t = t - DELAY
        over(EARLY, source_step)

        @pl.when(late_t % STRIDE == 0)
        def _():
            opened = late_t // STRIDE
            during(0, opened, chunks, lambda: pack(1, opened))

        over(NSTEP - EARLY, lambda i: source_step(i + EARLY))

        @pl.when(late_t == 0)
        def _():
            @pl.when(jnp.logical_not(home))
            def _():
                over(chunks, lambda c: speed_swap(c).wait_send())

        def receiver_step(i):
            k = NSTEP - STRIDE * i - (late_t + 1) % STRIDE
            c = (late_t - k + 1) // STRIDE

            def act():
                @pl.when(k == 1)
                def _():
                    clear_total(c)

                    @pl.when(c < chunks)
                    def _():
                        field_arrived(3, c)

                        @pl.when(jnp.logical_not(home) & (c + WINDOW < chunks))
                        def _():
                            field_swap(2, c + WINDOW).start()
                            field_swap(3, c + WINDOW).start()

                step(1, k, c)

                @pl.when((k == NSTEP) & (c > 0))
                def _():
                    @pl.when(home)
                    def _():
                        image_local(c - 1).start()

                    @pl.when(jnp.logical_not(home))
                    def _():
                        image_home(c - 1).start()

            during(0, c, chunks + 1, act)

        over(NSTEP // STRIDE, receiver_step)


        def pass_on(q):
            @pl.when(home)
            def _():
                image_local(q).wait()

            @pl.when(jnp.logical_not(home))
            def _():
                image_home(q).wait_recv()

            image_partner(q).start()
            y = chunk_at(q) * B
            L[0, pl.ds(GROUP + y, B)] = G[0, pl.ds(y, B)]

        def relay(q):
            image_partner(q).wait_recv()
            y = chunk_at(q) * B
            L[1, pl.ds(GROUP + y, B)] = G[1, pl.ds(y, B)]
            per_block = block // B
            e = chunk_at(q) % per_block

            @pl.when(chunk_at(q) // per_block == core)
            def _():
                for g in range(B // GROUP):
                    X[pl.ds(e * B + g * GROUP, GROUP)] = share(across, e * B + g * GROUP)
                image_across(e).start()

        def every(v, act):
            @pl.when(v % STRIDE == 0)
            def _():
                during(0, v // STRIDE, chunks, lambda: act(v // STRIDE))

        made = late_t - (NSTEP - 1) - STRIDE - LAG_A
        every(made, pass_on)
        every(made - LAG_B, relay)

    over(DELAY + NSTEP + STRIDE * chunks + LAG_A + LAG_B, slot_work)

    def collect(e):
        image_across(e).wait_recv()
        for g in range(B // GROUP):
            y = e * B + g * GROUP
            out_ref[pl.ds(y, GROUP)] = share(shot, y) + Y[pl.ds(y, GROUP)]

    per_block = block // B
    over(per_block, lambda i: collect(i * (1 - downward) + (per_block - 1 - i) * downward))

    @pl.when(jnp.logical_not(home))
    def _():
        image_home(chunks - 1).wait_send()

    image_partner(chunks - 1).wait_send()
    over(block // B, lambda e: image_across(e).wait_send())


def waves(anchors, traces, dest, rec_pos, now, prev, last, late, speed_model):
    rows, _, _, depth = now.shape
    block = speed_model.shape[0]
    shots, slabs = lax.axis_size("shot"), lax.axis_size("slab")
    chunks = rows // B
    padded = TOP + rows + TOP
    anywhere = pl.BlockSpec(memory_space=pl.ANY)
    dma = pltpu.SemaphoreType.DMA
    edge_all = 2 * (rows + 2 * B)
    return pl.pallas_call(
        wave_kernel,
        out_shape=jax.ShapeDtypeStruct((block, 2, 8, depth), jnp.float32),
        in_specs=[pl.BlockSpec(memory_space=pltpu.SMEM)]
        + [pl.BlockSpec(memory_space=pltpu.VMEM)] * 3
        + [anywhere] * 5,
        out_specs=pl.BlockSpec(memory_space=pltpu.VMEM),
        scratch_shapes=[
            pltpu.VMEM((NSTEP + 2, padded, 2, 8, depth), jnp.float32),
            pltpu.VMEM((NSTEP + 2, 2, edge_all, depth), jnp.float32),
            pltpu.VMEM((NSTEP, 2, edge_all, depth), jnp.float32),
            pltpu.VMEM((padded, 2, 8, depth), jnp.float32),
            pltpu.VMEM((padded, 2, 8, depth), jnp.float32),
            pltpu.VMEM((block * shots, 2, 8, depth), jnp.float32),
            pltpu.VMEM((2, rows, 2, 8, depth), jnp.float32),
            pltpu.VMEM((2, rows + 2 * GROUP, 2, 8, depth), jnp.float32),
            pltpu.VMEM((block, 2, 8, depth), jnp.float32),
            pltpu.VMEM((block, 2, 8, depth), jnp.float32),
            pltpu.VMEM((2 * depth, depth), jnp.bfloat16),
            pltpu.VMEM((slabs, shots * CAP, depth), jnp.float32),
            pltpu.VMEM((shots, slabs, shots * CAP, depth), jnp.float32),
            dma((2,)),
            dma((4, chunks)),
            dma((4, chunks)),
            dma((chunks,)),
            dma((chunks,)),
            dma((2, NSTEP, 2, chunks + 1)),
            dma((2, NSTEP, 2, chunks + 1)),
            dma((3, PIECES)),
            dma((3, PIECES)),
            dma((slabs,)),
            dma((slabs,)),
            dma((shots,)),
            dma((shots,)),
            dma((3, chunks)),
            dma((3, chunks)),
        ],
        compiler_params=pltpu.CompilerParams(
            collective_id=0, has_side_effects=True, vmem_limit_bytes=61 * 1024 * 1024
        ),
        name="waves",
    )(anchors, traces, dest, rec_pos, now, prev, last, late, speed_model)


def per_device(fwd_prev, fwd_now, adj_late, adj_last, speed_model, anchors, traces, dest, rec_pos):
    def halves(array):
        return array.reshape(array.shape[-3], 2, 8, array.shape[-1])

    image = waves(
        anchors, traces, dest.reshape(1, -1), rec_pos.reshape(1, -1),
        halves(fwd_now), halves(fwd_prev), halves(adj_last), halves(adj_late),
        halves(speed_model),
    )
    return image.reshape(speed_model.shape)


def solution(mesh):
    placed = (
        P("shot", None, "slab", None),
        P("shot", None, "slab", None),
        P("shot", None, "slab", None),
        P("shot", None, "slab", None),
        P("shot", "slab", None),
        P(),
        P(None, ("shot", "slab")),
        P(("shot", "slab"), None),
        P(("shot", "slab")),
    )
    return jax.shard_map(
        per_device, mesh=mesh, in_specs=placed, out_specs=P("shot", "slab", None), check_vma=False
    )
```
